32 devices in a mesh: liq: 4 (over y, x), ill: 2 (over core), dur: 4 (over z).
Axes of the slice: x: 2, y: 2, z: 4, core: 2. Of those that a mesh axis runs over, the one named last changes fastest.
Arguments:
- marginal_value: float32 [32, 8, 4, 512], P(None, 'dur', 'ill', 'liq'), may hold values from 0.5 to 2
- transition: float32 [32, 32], replicated, may hold values from 0 to 1, as said below
- discount_shock: float32 [32], replicated, may hold values from 0.5 to 2
- illiquid_drift: float32 [4], P('ill'), may hold values from 0.2 to 0.8
- durable_keep: float32 [8], P('dur'), may hold values from 0.3 to 0.9
- bracket_index: int32 [32, 8, 4, 512], P(None, 'dur', 'ill', 'liq'), may hold values from 0 to 510
- bracket_weight: float32 [32, 8, 4, 512], P(None, 'dur', 'ill', 'liq'), may hold values from 0 to 1
- steady_consumption: float32 [32, 8, 4, 512], P(None, 'dur', 'ill', 'liq'), may hold values from 0.8 to 1.6
- lottery_weight: float32 [32, 8, 4, 512], P(None, 'dur', 'ill', 'liq'), may hold values from 0 to 1
- liquid_target: int32 [32, 8, 4, 512], P(None, 'dur', 'ill', 'liq'), may hold values from 0 to 510
- illiquid_target: int32 [32, 8, 4], P(None, 'dur', 'ill'), may hold values from 0 to 3
- population: float32 [32, 8, 4, 512], P(None, 'dur', 'ill', 'liq'), may hold values from 0.5 to 2
Outputs:
- consumption: float32 [32, 8, 4, 512], P(None, 'dur', 'ill', 'liq')
- population_next: float32 [32, 8, 4, 512], P(None, 'dur', 'ill', 'liq')
The draws below stay inside these ranges and needn't reach their ends.
Inputs may be any that keep to these rules, and one draw needn't show every extreme that they name: `bracket_index`: global liquid index; the upper bracket point is index + 1. `liquid_target`: global liquid index; the upper target is index + 1. `illiquid_target`: global illiquid index. `transition`: entries positive, every row sums to one.
All inputs are finite; a program needn't handle non-finite values.
Results may differ from the reference program's by a relative error of at most 0.000065.
Values sent between devices are 32-bit elements; how exact they have to be, the bound alone decides.
A program may use at most 64 MiB of HBM per device.

```python
import math
import jax
import jax.numpy as jnp
from jax import lax

Z = 32
NB = 512
NA = 4
ND = 8


def draw_transition(key, part):
    key_spread, key_diagonal = jax.random.split(key)
    spread = jax.random.uniform(key_spread, (Z, Z), jnp.float32, 0.2, 1.0)
    diagonal = jax.random.uniform(key_diagonal, (Z,), jnp.float32, 20.0, 30.0)
    raw_matrix = spread + jnp.diag(diagonal)
    return raw_matrix / jnp.sum(raw_matrix, axis=1, keepdims=True)


def place_ends(array, stream_key, low, top_value):
    extent = array.shape
    index_at = [jax.random.randint(jax.random.fold_in(stream_key, axis), (), 0, extent[axis]) for axis in range(len(extent))]
    array = array.at[tuple(index_at)].set(low)
    longest = extent.index(max(extent))
    index_at[longest] = (index_at[longest] + 1) % extent[longest]
    return array.at[tuple(index_at)].set(top_value)


def block_levels(stream_key, dims, pieces, least, high):
    level, own = 1.0, jax.random.fold_in(stream_key, 6)
    for position, shards_of in pieces:
        heights = jnp.exp(jax.random.uniform(jax.random.fold_in(own, position), (shards_of,), jnp.float32, least / len(pieces), high / len(pieces)))
        level = level * jnp.repeat(heights, dims[position] // shards_of).reshape([-1 if axis == position else 1 for axis in range(len(dims))])
    return level


def setup_inputs(seed: int = 0) -> dict:
    key_list = jax.random.split(jax.random.key(seed), 13)
    return {
        "marginal_value": jnp.clip(jnp.exp(math.log(2.0) - 1.3862944 * jax.random.uniform(key_list[0], (Z, ND, NA, NB), jnp.float32) ** block_levels(key_list[0], (Z, ND, NA, NB), ((1, 4), (2, 2), (3, 4)), -0.2, 0.2)), 0.5, 2.0),
        "transition": draw_transition(jax.random.fold_in(key_list[12], 71), 0),
        "discount_shock": jnp.clip(jnp.exp(jax.random.uniform(key_list[2], (Z,), jnp.float32, math.log(0.5), math.log(2.0))), 0.5, 2.0),
        "illiquid_drift": jnp.clip(0.2 + 0.6 * jax.random.uniform(key_list[3], (NA,), jnp.float32) ** block_levels(key_list[3], (NA,), ((0, 2),), -0.2, 0.2), 0.2, 0.8),
        "durable_keep": jnp.clip(0.3 + 0.59999996 * jax.random.uniform(key_list[4], (ND,), jnp.float32) ** block_levels(key_list[4], (ND,), ((0, 4),), -0.2, 0.2), 0.3, 0.9),
        "bracket_index": place_ends(jax.random.randint(key_list[5], (Z, ND, NA, NB), 0, NB - 1), jax.random.fold_in(key_list[5], 1), 0, (NB - 1) - 1).astype(jnp.int32),
        "bracket_weight": jnp.clip(1.0 * jax.random.uniform(key_list[6], (Z, ND, NA, NB), jnp.float32) ** block_levels(key_list[6], (Z, ND, NA, NB), ((1, 4), (2, 2), (3, 4)), -0.2, 0.2), 0.0, 1.0),
        "steady_consumption": jnp.clip(0.8 + 0.8 * jax.random.uniform(key_list[7], (Z, ND, NA, NB), jnp.float32) ** block_levels(key_list[7], (Z, ND, NA, NB), ((1, 4), (2, 2), (3, 4)), -0.2, 0.2), 0.8, 1.6),
        "lottery_weight": jnp.clip(1.0 * jax.random.uniform(key_list[8], (Z, ND, NA, NB), jnp.float32) ** block_levels(key_list[8], (Z, ND, NA, NB), ((1, 4), (2, 2), (3, 4)), -0.2, 0.2), 0.0, 1.0),
        "liquid_target": place_ends(jax.random.randint(key_list[9], (Z, ND, NA, NB), 0, NB - 1), jax.random.fold_in(key_list[9], 1), 0, (NB - 1) - 1).astype(jnp.int32),
        "illiquid_target": place_ends(jax.random.randint(key_list[10], (Z, ND, NA), 0, NA), jax.random.fold_in(key_list[10], 1), 0, NA - 1).astype(jnp.int32),
        "population": jnp.clip(jnp.exp(math.log(2.0) - 1.3862944 * jax.random.uniform(key_list[11], (Z, ND, NA, NB), jnp.float32) ** block_levels(key_list[11], (Z, ND, NA, NB), ((1, 4), (2, 2), (3, 4)), -0.2, 0.2)), 0.5, 2.0),
    }


DISCOUNT = 0.96
GROSS_RATE = 1.01
SLOPE_GAIN = 0.5
HIGHEST_PREC = lax.Precision.HIGHEST

def expect_upper(values, transition, drift_rate):
    expected = jnp.einsum('zy,ydab->zdab', transition, values, precision=HIGHEST_PREC)
    upper_plane = jnp.concatenate([expected[:, :, 1:, :], expected[:, :, -1:, :]], axis=2)
    drift_full = drift_rate[None, None, :, None]
    return drift_full * expected + (1.0 - drift_full) * upper_plane

def backward_step(values, transition, drift_rate, shock_scale, bracket_index, bracket_weight):
    drifted = expect_upper(values, transition, drift_rate)
    endogenous = lax.rsqrt(DISCOUNT * GROSS_RATE * shock_scale[:, None, None, None] * drifted)
    lower_value = jnp.take_along_axis(endogenous, bracket_index, axis=3)
    upper_value = jnp.take_along_axis(endogenous, bracket_index + 1, axis=3)
    return bracket_weight * lower_value + (1.0 - bracket_weight) * upper_value

def reference(marginal_value, transition, discount_shock, illiquid_drift, durable_keep, bracket_index, bracket_weight, steady_consumption, lottery_weight, liquid_target, illiquid_target, population):
    policy_one = backward_step(marginal_value, transition, illiquid_drift, discount_shock, bracket_index, bracket_weight)
    value_two = GROSS_RATE / (policy_one * policy_one)
    consumption = backward_step(value_two, transition, illiquid_drift, jnp.ones_like(discount_shock), bracket_index, bracket_weight)
    share = jnp.clip(lottery_weight + SLOPE_GAIN * (policy_one - steady_consumption), 0.0, 1.0)
    incomes, durables, ill_count, liq_count = population.shape
    inc_idx = lax.broadcasted_iota(jnp.int32, population.shape, 0)
    dur_idx = lax.broadcasted_iota(jnp.int32, population.shape, 1)
    ill_dest = jnp.broadcast_to(illiquid_target[:, :, :, None], population.shape).astype(jnp.int32)
    base_index = ((inc_idx * durables + dur_idx) * ill_count + ill_dest) * liq_count
    flat_mass = jnp.zeros((incomes * durables * ill_count * liq_count,), jnp.float32)
    flat_mass = flat_mass.at[(base_index + liquid_target).reshape(-1)].add((population * share).reshape(-1))
    flat_mass = flat_mass.at[(base_index + liquid_target + 1).reshape(-1)].add((population * (1.0 - share)).reshape(-1))
    lottery_mass = flat_mass.reshape(population.shape)
    dur_plane = lax.broadcasted_iota(jnp.int32, (durables,), 0)
    stay_share = jnp.where(dur_plane == 0, 1.0, durable_keep)[None, :, None, None]
    depart = (1.0 - stay_share) * lottery_mass
    settled = stay_share * lottery_mass + jnp.concatenate([depart[:, 1:], jnp.zeros_like(depart[:, :1])], axis=1)
    population_next = jnp.einsum('zy,zdab->ydab', transition, settled, precision=HIGHEST_PREC)
    return (consumption, population_next)
```

```python
import functools

import jax
import jax.numpy as jnp
from jax import lax
from jax.experimental import pallas as pl
from jax.experimental.pallas import tpu as pltpu
from jax.sharding import PartitionSpec as P

DISCOUNT = 0.96
GROSS_RATE = 1.01
SLOPE_GAIN = 0.5
HIGHEST_PREC = lax.Precision.HIGHEST
MESH_ID = pl.DeviceIdType.MESH
NT = (((1,), (1,)), ((), ()))
TILE = 8


def split_by(x, n):
    if n & (n - 1) == 0:
        return x >> (n.bit_length() - 1), x & (n - 1)
    return lax.div(x, jnp.int32(n)), lax.rem(x, jnp.int32(n))


def dot(a, b):
    return jnp.dot(a, b, precision=HIGHEST_PREC, preferred_element_type=jnp.float32)


def iota(shape, axis):
    return lax.broadcasted_iota(jnp.int32, shape, axis)


def as_float(flag):
    return jnp.where(flag, jnp.float32(1.0), jnp.float32(0.0))


def kernel(
    dims,
    value_ref, transition_ref, shock_ref, drift_ref, keep_ref, index_ref, weight_ref,
    steady_ref, lottery_ref, target_ref, ill_target_ref, population_ref,
    consumption_ref, next_ref,
    first_mat, first_up, second_mat, second_up, next_mat, next_in,
    near_value, value_two, pencil, policy, mass_low, mass_high, target_hi, target_lo,
    terms, terms_in, owner_sum, owner_in, settled, depart, depart_in,
    value_send, value_recv, pencil_send, pencil_recv, terms_send, terms_recv,
    owner_send, owner_recv, depart_send, depart_recv,
):
    incomes, durables, ill_rows, liq_rows, liq_n, ill_n, dur_n = dims
    group = durables * ill_rows
    rows = incomes * group
    plane_rows = incomes * ill_rows
    liq_me, ill_me, dur_me = (lax.axis_index(name) for name in ("liq", "ill", "dur"))

    barrier = pltpu.get_barrier_semaphore()
    for step in range(1, liq_n):
        pl.semaphore_signal(barrier, inc=1, device_id={"liq": lax.rem(liq_me + step, liq_n)}, device_id_type=MESH_ID)
    for step in range(1, ill_n):
        pl.semaphore_signal(barrier, inc=1, device_id={"ill": lax.rem(ill_me + step, ill_n)}, device_id_type=MESH_ID)

    @pl.when(dur_me > 0)
    def _():
        pl.semaphore_signal(barrier, inc=1, device_id={"dur": dur_me - 1}, device_id_type=MESH_ID)

    @pl.when(dur_me < dur_n - 1)
    def _():
        pl.semaphore_signal(barrier, inc=1, device_id={"dur": dur_me + 1}, device_id_type=MESH_ID)

    dur_peers = jnp.minimum(dur_me, 1) + jnp.minimum(dur_n - 1 - dur_me, 1)
    pl.semaphore_wait(barrier, liq_n - 1 + ill_n - 1 + dur_peers)

    ill_below = lax.rem(ill_me + ill_n - 1, ill_n)

    def value_copy(k, source):
        return pltpu.make_async_remote_copy(
            src_ref=source, dst_ref=near_value.at[k], send_sem=value_send.at[k],
            recv_sem=value_recv.at[k], device_id={"ill": ill_below}, device_id_type=MESH_ID,
        )

    def pencil_copy(k, step):
        peer = lax.rem(liq_me + step, liq_n)
        return pltpu.make_async_remote_copy(
            src_ref=pencil.at[k * liq_n + liq_me], dst_ref=pencil.at[k * liq_n + liq_me],
            send_sem=pencil_send.at[k * liq_n + step], recv_sem=pencil_recv.at[k * liq_n + step],
            device_id={"liq": peer}, device_id_type=MESH_ID,
        )

    def terms_copy(step):
        peer = lax.rem(ill_me + step, ill_n)
        return pltpu.make_async_remote_copy(
            src_ref=terms.at[pl.ds(peer * (liq_n * rows), liq_n * rows)], dst_ref=terms_in.at[step - 1],
            send_sem=terms_send.at[step - 1], recv_sem=terms_recv.at[step - 1],
            device_id={"ill": peer}, device_id_type=MESH_ID,
        )

    def owner_copy(step):
        peer = lax.rem(liq_me + step, liq_n)
        return pltpu.make_async_remote_copy(
            src_ref=owner_sum.at[peer], dst_ref=owner_in.at[step - 1],
            send_sem=owner_send.at[step - 1], recv_sem=owner_recv.at[step - 1],
            device_id={"liq": peer}, device_id_type=MESH_ID,
        )

    value_copy(0, value_ref).start()

    transition = transition_ref[...]
    row_z, row_rest = split_by(iota((rows, rows), 0), group)
    col_z, col_rest = split_by(iota((rows, rows), 1), group)
    row_d, row_a = split_by(row_rest, ill_rows)
    col_d, col_a = split_by(col_rest, ill_rows)
    spread = as_float(split_by(iota((rows, incomes), 0), group)[0] == iota((rows, incomes), 1))
    spread_t = as_float(iota((incomes, rows), 0) == split_by(iota((incomes, rows), 1), group)[0])
    drift = jnp.zeros((rows, rows), jnp.float32)
    for a in range(ill_rows):
        drift = jnp.where(row_a == a, drift_ref[a], drift)
    is_last = as_float(ill_me == ill_n - 1)
    same_d = row_d == col_d
    top_row = row_a == ill_rows - 1
    local = jnp.where(col_a == row_a, drift, 0.0)
    local = local + jnp.where(col_a == row_a + 1, 1.0 - drift, 0.0)
    local = local + jnp.where(top_row & (col_a == ill_rows - 1), is_last * (1.0 - drift), 0.0)
    local = jnp.where(same_d, local, 0.0)
    upper = jnp.where(same_d & top_row & (col_a == 0), (1.0 - is_last) * (1.0 - drift), 0.0)
    constant = jnp.float32(DISCOUNT * GROSS_RATE)
    eye = iota((incomes, incomes), 0) == iota((incomes, incomes), 1)
    scaled = dot(jnp.where(eye, constant * shock_ref[...], 0.0), transition)
    wide = dot(dot(spread, scaled), spread_t)
    first_mat[...] = wide * local
    first_up[...] = wide * upper

    value_copy(0, value_ref).wait_recv()
    drifted = dot(first_mat[...], value_ref[...]) + dot(first_up[...], near_value[0])
    pencil[liq_me] = lax.rsqrt(drifted)
    for step in range(1, liq_n):
        pencil_copy(0, step).start()

    wide = constant * dot(dot(spread, transition), spread_t)
    second_mat[...] = wide * local
    second_up[...] = wide * upper

    first_d = as_float(dur_me == 0)
    stay = [keep_ref[d] for d in range(durables)]
    stay[0] = first_d + (1.0 - first_d) * stay[0]
    back_d, back_rest = split_by(iota((rows, rows), 1), plane_rows)
    back_a = split_by(back_rest, ill_rows)[1]
    stays = jnp.zeros((rows, rows), jnp.float32)
    for d in range(durables):
        stays = jnp.where(back_d == d, stay[d], stays)
    mix = jnp.where(back_d == row_d, stays, 0.0) + jnp.where(back_d == row_d + 1, 1.0 - stays, 0.0)
    mix = jnp.where(back_a == row_a, mix, 0.0)
    back_z = split_by(split_by(iota((incomes, rows), 1), plane_rows)[1], ill_rows)[0]
    turned = lax.dot_general(spread, transition, NT, precision=HIGHEST_PREC, preferred_element_type=jnp.float32)
    wide = dot(turned, as_float(iota((incomes, rows), 0) == back_z))
    next_mat[...] = wide * mix
    in_z, in_a = split_by(iota((incomes, plane_rows), 1), ill_rows)
    wide = dot(turned, as_float(iota((incomes, plane_rows), 0) == in_z))
    in_row = split_by(iota((rows, plane_rows), 0), group)[1]
    in_row_d, in_row_a = split_by(in_row, ill_rows)
    in_col_a = split_by(iota((rows, plane_rows), 1), ill_rows)[1]
    next_in[...] = jnp.where((in_row_d == durables - 1) & (in_row_a == in_col_a), wide, 0.0)

    def block_of(position):
        block = jnp.zeros(position.shape, jnp.int32)
        for h in range(1, liq_n):
            block = block + jnp.where(position >= h * liq_rows, 1, 0)
        return block, position - block * liq_rows

    target = target_ref[...]
    target_hi[...], target_lo[...] = block_of(target)

    def interpolate(k, tile):
        span = pl.ds(tile * TILE, TILE)
        index = index_ref[span, :]
        low_block, low_lane = block_of(index)
        high_block, high_lane = block_of(index + 1)
        low = high = None
        for h in range(liq_n):
            block = pencil[k * liq_n + h, span, :]
            low_h = jnp.take_along_axis(block, low_lane, axis=1, mode="promise_in_bounds")
            high_h = jnp.take_along_axis(block, high_lane, axis=1, mode="promise_in_bounds")
            low = low_h if h == 0 else jnp.where(low_block == h, low_h, low)
            high = high_h if h == 0 else jnp.where(high_block == h, high_h, high)
        weight = weight_ref[span, :]
        return weight * low + (1.0 - weight) * high

    for step in range(1, liq_n):
        pencil_copy(0, step).wait_recv()
    for tile in range(rows // TILE):
        span = pl.ds(tile * TILE, TILE)
        chosen = interpolate(0, tile)
        policy[span, :] = chosen
        value_two[span, :] = GROSS_RATE / (chosen * chosen)
    value_copy(1, value_two).start()

    share = jnp.clip(lottery_ref[...] + SLOPE_GAIN * (policy[...] - steady_ref[...]), 0.0, 1.0)
    mass = population_ref[...]
    mass_low[...] = mass * share
    mass_high[...] = mass * (1.0 - share)

    lanes = 2 * liq_n
    sub = iota((lanes, liq_rows), 0)
    lane = iota((lanes, liq_rows), 1)
    sub_block = jnp.where(sub < liq_n, sub, sub - liq_n)
    lane_row = iota((liq_rows, liq_rows), 0)
    per_tile = TILE // group

    def scatter_tile(tile, carry):
        span = pl.ds(pl.multiple_of(tile * TILE, TILE), TILE)
        low_t, high_t, hi_t, lo_t = mass_low[span, :], mass_high[span, :], target_hi[span, :], target_lo[span, :]
        for zz in range(per_tile):
            z = tile * per_tile + zz
            for d in range(durables):
                totals = []
                for a in range(ill_rows):
                    k = zz * group + d * ill_rows + a
                    both = jnp.where(sub < liq_n, low_t[k : k + 1, :], high_t[k : k + 1, :])
                    both = jnp.where(hi_t[k : k + 1, :] == sub_block, both, 0.0)
                    rounded = both.astype(jnp.bfloat16).astype(jnp.float32)
                    parts = jnp.concatenate([both, both - rounded], axis=0).astype(jnp.bfloat16)
                    hot = as_float(lane_row == lo_t[k : k + 1, :]).astype(jnp.bfloat16)
                    placed = lax.dot_general(parts, hot, NT, preferred_element_type=jnp.float32)
                    placed = placed[:lanes] + placed[lanes:]
                    moved = pltpu.roll(placed, 1, 1)
                    same = pltpu.roll(moved, liq_n, 0)
                    prior = pltpu.roll(moved, liq_n + 1, 0)
                    totals.append(placed + jnp.where(lane > 0, same, jnp.where(sub > 0, prior, 0.0)))
                for dest in range(ill_n * ill_rows):
                    out = None
                    for a in range(ill_rows):
                        here = as_float(ill_target_ref[d * ill_rows + a, z] == dest) * totals[a]
                        out = here if out is None else out + here
                    base = (dest // ill_rows) * liq_n * rows + d * plane_rows + z * ill_rows + dest % ill_rows
                    terms[pl.ds(base, liq_n, stride=rows), :] = out[:liq_n]
        return carry

    tiles = rows // TILE
    lax.fori_loop(0, tiles // 2, scatter_tile, 0)

    value_copy(1, value_two).wait_recv()
    drifted = dot(second_mat[...], value_two[...]) + dot(second_up[...], near_value[1])
    pencil[liq_n + liq_me] = lax.rsqrt(drifted)
    for step in range(1, liq_n):
        pencil_copy(1, step).start()

    lax.fori_loop(tiles // 2, tiles, scatter_tile, 0)
    for step in range(1, ill_n):
        terms_copy(step).start()
    for step in range(1, ill_n):
        terms_copy(step).wait_recv()
    for h in range(liq_n):
        total = terms[pl.ds(pl.multiple_of((ill_me * liq_n + h) * rows, TILE), rows), :]
        for step in range(1, ill_n):
            total = total + terms_in[step - 1, pl.ds(h * rows, rows), :]
        owner_sum[h] = total
    for step in range(1, liq_n):
        owner_copy(step).start()

    for step in range(1, liq_n):
        pencil_copy(1, step).wait_recv()
    for tile in range(rows // TILE):
        consumption_ref[pl.ds(tile * TILE, TILE), :] = interpolate(1, tile)

    for step in range(1, liq_n):
        owner_copy(step).wait_recv()
    total = owner_sum[liq_me]
    for step in range(1, liq_n):
        total = total + owner_in[step - 1]
    settled[...] = total
    depart[...] = (1.0 - stay[0]) * total[:plane_rows]

    depart_copy = pltpu.make_async_remote_copy(
        src_ref=depart, dst_ref=depart_in, send_sem=depart_send.at[0], recv_sem=depart_recv.at[0],
        device_id={"dur": jnp.maximum(dur_me - 1, 0)}, device_id_type=MESH_ID,
    )

    @pl.when(dur_me > 0)
    def _():
        depart_copy.start()

    next_ref[...] = dot(next_mat[...], settled[...])

    @pl.when(dur_me < dur_n - 1)
    def _():
        depart_copy.wait_recv()
        next_ref[...] += dot(next_in[...], depart_in[...])

    value_copy(0, value_ref).wait_send()
    value_copy(1, value_two).wait_send()
    for step in range(1, liq_n):
        pencil_copy(0, step).wait_send()
        pencil_copy(1, step).wait_send()
        owner_copy(step).wait_send()
    for step in range(1, ill_n):
        terms_copy(step).wait_send()

    @pl.when(dur_me > 0)
    def _():
        depart_copy.wait_send()


def body(
    marginal_value,
    transition,
    discount_shock,
    illiquid_drift,
    durable_keep,
    bracket_index,
    bracket_weight,
    steady_consumption,
    lottery_weight,
    liquid_target,
    illiquid_target,
    population,
):
    shape = marginal_value.shape
    incomes, durables, ill_rows, liq_rows = shape
    liq_n, ill_n, dur_n = (lax.axis_size(name) for name in ("liq", "ill", "dur"))
    rows = incomes * durables * ill_rows
    plane_rows = incomes * ill_rows
    flat = lambda x: x.reshape(rows, liq_rows)
    vmem = pl.BlockSpec(memory_space=pltpu.VMEM)
    smem = pl.BlockSpec(memory_space=pltpu.SMEM)
    f32 = jnp.float32
    block = (rows, liq_rows)
    dma = pltpu.SemaphoreType.DMA
    result = jax.ShapeDtypeStruct(block, f32)
    dims = (incomes, durables, ill_rows, liq_rows, liq_n, ill_n, dur_n)
    outs = pl.pallas_call(
        functools.partial(kernel, dims),
        out_shape=(result, result),
        in_specs=[vmem, vmem, vmem, smem, smem, vmem, vmem, vmem, vmem, vmem, smem, vmem],
        out_specs=(vmem, vmem),
        scratch_shapes=[
            pltpu.VMEM((rows, rows), f32),
            pltpu.VMEM((rows, rows), f32),
            pltpu.VMEM((rows, rows), f32),
            pltpu.VMEM((rows, rows), f32),
            pltpu.VMEM((rows, rows), f32),
            pltpu.VMEM((rows, plane_rows), f32),
            pltpu.VMEM((2,) + block, f32),
            pltpu.VMEM(block, f32),
            pltpu.VMEM((2 * liq_n,) + block, f32),
            pltpu.VMEM(block, f32),
            pltpu.VMEM(block, f32),
            pltpu.VMEM(block, f32),
            pltpu.VMEM(block, jnp.int32),
            pltpu.VMEM(block, jnp.int32),
            pltpu.VMEM((ill_n * liq_n * rows, liq_rows), f32),
            pltpu.VMEM((ill_n - 1, liq_n * rows, liq_rows), f32),
            pltpu.VMEM((liq_n,) + block, f32),
            pltpu.VMEM((liq_n - 1,) + block, f32),
            pltpu.VMEM(block, f32),
            pltpu.VMEM((plane_rows, liq_rows), f32),
            pltpu.VMEM((plane_rows, liq_rows), f32),
            dma((2,)),
            dma((2,)),
            dma((2 * liq_n,)),
            dma((2 * liq_n,)),
            dma((ill_n - 1,)),
            dma((ill_n - 1,)),
            dma((liq_n - 1,)),
            dma((liq_n - 1,)),
            dma((1,)),
            dma((1,)),
        ],
        compiler_params=pltpu.CompilerParams(collective_id=0, has_side_effects=True),
        name="window",
    )(
        flat(marginal_value),
        transition,
        discount_shock.reshape(1, incomes),
        illiquid_drift,
        durable_keep,
        flat(bracket_index),
        flat(bracket_weight),
        flat(steady_consumption),
        flat(lottery_weight),
        flat(liquid_target),
        jnp.transpose(illiquid_target, (1, 2, 0)).reshape(durables * ill_rows, incomes),
        flat(population),
    )
    return tuple(out.reshape(shape) for out in outs)


def solution(mesh):
    in_specs = (
        P(None, "dur", "ill", "liq"),
        P(),
        P(),
        P("ill"),
        P("dur"),
        P(None, "dur", "ill", "liq"),
        P(None, "dur", "ill", "liq"),
        P(None, "dur", "ill", "liq"),
        P(None, "dur", "ill", "liq"),
        P(None, "dur", "ill", "liq"),
        P(None, "dur", "ill"),
        P(None, "dur", "ill", "liq"),
    )
    out_specs = (P(None, "dur", "ill", "liq"), P(None, "dur", "ill", "liq"))
    return jax.shard_map(body, mesh=mesh, in_specs=in_specs, out_specs=out_specs, check_vma=False)
```

```python
import functools

import jax
import jax.numpy as jnp
from jax import lax
from jax.experimental import pallas as pl
from jax.experimental.pallas import tpu as pltpu
from jax.sharding import PartitionSpec as P

DISCOUNT = 0.96
GROSS_RATE = 1.01
SLOPE_GAIN = 0.5
HIGHEST_PREC = lax.Precision.HIGHEST
MESH_ID = pl.DeviceIdType.MESH
NT = (((1,), (1,)), ((), ()))
TILE = 8


def split_by(x, n):
    if n & (n - 1) == 0:
        return x >> (n.bit_length() - 1), x & (n - 1)
    return lax.div(x, jnp.int32(n)), lax.rem(x, jnp.int32(n))


def dot(a, b):
    return jnp.dot(a, b, precision=HIGHEST_PREC, preferred_element_type=jnp.float32)


def iota(shape, axis):
    return lax.broadcasted_iota(jnp.int32, shape, axis)


def as_float(flag):
    return jnp.where(flag, jnp.float32(1.0), jnp.float32(0.0))


def peer_of(me, step, n):
    if n & (n - 1):
        return lax.rem(me + step, n)
    out = me
    for bit in range(n.bit_length() - 1):
        if step >> bit & 1:
            out = out + (1 - 2 * lax.rem(lax.div(me, jnp.int32(1 << bit)), jnp.int32(2))) * (1 << bit)
    return out


def kernel(
    dims,
    value_hbm, transition_hbm, shock_hbm, drift_ref, keep_ref, index_hbm, weight_hbm,
    steady_hbm, lottery_hbm, target_hbm, ill_target_ref, population_hbm,
    consumption_hbm, next_hbm,
    value_ref, transition_ref, shock_ref, index_ref, weight_ref, steady_ref, lottery_ref, target_ref,
    population_ref, consumption_ref, next_ref, load_sem, store_sem,
    first_mat, first_up, second_mat, second_up, next_mat, next_in,
    near_value, value_two, pencil, mass_low, mass_high, target_hi, target_lo,
    terms, terms_in, owner_sum, owner_in, settled, depart, depart_in,
    value_send, value_recv, pencil_send, pencil_recv, terms_send, terms_recv,
    owner_send, owner_recv, depart_send, depart_recv,
):
    incomes, durables, ill_rows, liq_rows, liq_n, ill_n, dur_n = dims
    group = durables * ill_rows
    rows = incomes * group
    half_rows = rows // 2
    plane_rows = incomes * ill_rows
    liq_me, ill_me, dur_me = (lax.axis_index(name) for name in ("liq", "ill", "dur"))
    far_first = range(liq_n - 1, 0, -1)

    barrier = pltpu.get_barrier_semaphore()
    for step in far_first:
        pl.semaphore_signal(barrier, inc=1, device_id={"liq": peer_of(liq_me, step, liq_n)}, device_id_type=MESH_ID)
    for step in range(1, ill_n):
        pl.semaphore_signal(barrier, inc=1, device_id={"ill": peer_of(ill_me, step, ill_n)}, device_id_type=MESH_ID)

    @pl.when(dur_me > 0)
    def _():
        pl.semaphore_signal(barrier, inc=1, device_id={"dur": dur_me - 1}, device_id_type=MESH_ID)

    @pl.when(dur_me < dur_n - 1)
    def _():
        pl.semaphore_signal(barrier, inc=1, device_id={"dur": dur_me + 1}, device_id_type=MESH_ID)

    loads = [
        pltpu.make_async_copy(source, held, load_sem.at[slot])
        for slot, (source, held) in enumerate((
            (transition_hbm, transition_ref), (shock_hbm, shock_ref), (value_hbm, value_ref),
            (index_hbm, index_ref), (weight_hbm, weight_ref), (target_hbm, target_ref),
            (lottery_hbm, lottery_ref), (steady_hbm, steady_ref), (population_hbm, population_ref),
        ))
    ]
    for load in loads:
        load.start()
    loads[0].wait()
    loads[1].wait()

    transition = transition_ref[...]
    row_z, row_rest = split_by(iota((rows, rows), 0), group)
    col_z, col_rest = split_by(iota((rows, rows), 1), group)
    row_d, row_a = split_by(row_rest, ill_rows)
    col_d, col_a = split_by(col_rest, ill_rows)
    spread = as_float(split_by(iota((rows, incomes), 0), group)[0] == iota((rows, incomes), 1))
    spread_t = as_float(iota((incomes, rows), 0) == split_by(iota((incomes, rows), 1), group)[0])
    drift = jnp.zeros((rows, rows), jnp.float32)
    for a in range(ill_rows):
        drift = jnp.where(row_a == a, drift_ref[a], drift)
    is_last = as_float(ill_me == ill_n - 1)
    same_d = row_d == col_d
    top_row = row_a == ill_rows - 1
    local = jnp.where(col_a == row_a, drift, 0.0)
    local = local + jnp.where(col_a == row_a + 1, 1.0 - drift, 0.0)
    local = local + jnp.where(top_row & (col_a == ill_rows - 1), is_last * (1.0 - drift), 0.0)
    local = jnp.where(same_d, local, 0.0)
    upper = jnp.where(same_d & top_row & (col_a == 0), (1.0 - is_last) * (1.0 - drift), 0.0)
    constant = jnp.float32(DISCOUNT * GROSS_RATE)
    eye = iota((incomes, incomes), 0) == iota((incomes, incomes), 1)
    scaled = dot(jnp.where(eye, constant * shock_ref[...], 0.0), transition)
    wide = dot(dot(spread, scaled), spread_t)
    first_mat[...] = wide * local
    first_up[...] = wide * upper

    dur_peers = jnp.minimum(dur_me, 1) + jnp.minimum(dur_n - 1 - dur_me, 1)
    pl.semaphore_wait(barrier, liq_n - 1 + ill_n - 1 + dur_peers)

    ill_below = lax.rem(ill_me + ill_n - 1, ill_n)

    def value_copy(k, source):
        return pltpu.make_async_remote_copy(
            src_ref=source, dst_ref=near_value.at[k], send_sem=value_send.at[k],
            recv_sem=value_recv.at[k], device_id={"ill": ill_below}, device_id_type=MESH_ID,
        )

    def pencil_copy(k, half, step):
        slot = (k * 2 + half) * liq_n + step
        part = pencil.at[k * liq_n + liq_me, pl.ds(half * half_rows, half_rows)]
        return pltpu.make_async_remote_copy(
            src_ref=part, dst_ref=part, send_sem=pencil_send.at[slot], recv_sem=pencil_recv.at[slot],
            device_id={"liq": peer_of(liq_me, step, liq_n)}, device_id_type=MESH_ID,
        )

    def terms_copy(d, step):
        peer = peer_of(ill_me, step, ill_n)
        slot = d * (ill_n - 1) + step - 1
        return pltpu.make_async_remote_copy(
            src_ref=terms.at[pl.ds((d * ill_n + peer) * (liq_n * plane_rows), liq_n * plane_rows)],
            dst_ref=terms_in.at[slot], send_sem=terms_send.at[slot], recv_sem=terms_recv.at[slot],
            device_id={"ill": peer}, device_id_type=MESH_ID,
        )

    def owner_copy(d, step):
        peer = peer_of(liq_me, step, liq_n)
        slot = d * (liq_n - 1) + step - 1
        return pltpu.make_async_remote_copy(
            src_ref=owner_sum.at[d * liq_n + peer], dst_ref=owner_in.at[slot],
            send_sem=owner_send.at[slot], recv_sem=owner_recv.at[slot],
            device_id={"liq": peer}, device_id_type=MESH_ID,
        )

    loads[2].wait()
    value_copy(0, value_ref).start()
    drifted = dot(first_mat[...], value_ref[...])
    value_copy(0, value_ref).wait_recv()
    drifted = drifted + dot(first_up[...], near_value[0])
    pencil[liq_me] = lax.rsqrt(drifted)
    for half in range(2):
        for step in far_first:
            pencil_copy(0, half, step).start()

    wide = constant * dot(dot(spread, transition), spread_t)
    second_mat[...] = wide * local
    second_up[...] = wide * upper

    first_d = as_float(dur_me == 0)
    stay = [keep_ref[d] for d in range(durables)]
    stay[0] = first_d + (1.0 - first_d) * stay[0]
    back_d, back_rest = split_by(iota((rows, rows), 1), plane_rows)
    back_a = split_by(back_rest, ill_rows)[1]
    stays = jnp.zeros((rows, rows), jnp.float32)
    for d in range(durables):
        stays = jnp.where(back_d == d, stay[d], stays)
    mix = jnp.where(back_d == row_d, stays, 0.0) + jnp.where(back_d == row_d + 1, 1.0 - stays, 0.0)
    mix = jnp.where(back_a == row_a, mix, 0.0)
    back_z = split_by(split_by(iota((incomes, rows), 1), plane_rows)[1], ill_rows)[0]
    turned = lax.dot_general(spread, transition, NT, precision=HIGHEST_PREC, preferred_element_type=jnp.float32)
    wide = dot(turned, as_float(iota((incomes, rows), 0) == back_z))
    next_mat[...] = wide * mix
    in_z, in_a = split_by(iota((incomes, plane_rows), 1), ill_rows)
    wide = dot(turned, as_float(iota((incomes, plane_rows), 0) == in_z))
    in_row = split_by(iota((rows, plane_rows), 0), group)[1]
    in_row_d, in_row_a = split_by(in_row, ill_rows)
    in_col_a = split_by(iota((rows, plane_rows), 1), ill_rows)[1]
    next_in[...] = jnp.where((in_row_d == durables - 1) & (in_row_a == in_col_a), wide, 0.0)

    def block_of(position):
        block = jnp.zeros(position.shape, jnp.int32)
        for h in range(1, liq_n):
            block = block + jnp.where(position >= h * liq_rows, 1, 0)
        return block, position - block * liq_rows

    for load in loads[3:]:
        load.wait()
    target_hi[...], target_lo[...] = block_of(target_ref[...])

    def interpolate(k, tile):
        span = pl.ds(tile * TILE, TILE)
        index = index_ref[span, :]
        low_block, low_lane = block_of(index)
        high_block, high_lane = block_of(index + 1)
        low = high = None
        for h in range(liq_n):
            block = pencil[k * liq_n + h, span, :]
            low_h = jnp.take_along_axis(block, low_lane, axis=1, mode="promise_in_bounds")
            high_h = jnp.take_along_axis(block, high_lane, axis=1, mode="promise_in_bounds")
            low = low_h if h == 0 else jnp.where(low_block == h, low_h, low)
            high = high_h if h == 0 else jnp.where(high_block == h, high_h, high)
        weight = weight_ref[span, :]
        return weight * low + (1.0 - weight) * high

    tiles = rows // TILE
    halves = (range(tiles // 2), range(tiles // 2, tiles))

    def first_policy(half):
        for step in far_first:
            pencil_copy(0, half, step).wait_recv()
        for tile in halves[half]:
            span = pl.ds(tile * TILE, TILE)
            chosen = interpolate(0, tile)
            value_two[span, :] = GROSS_RATE / (chosen * chosen)
            share = jnp.clip(lottery_ref[span, :] + SLOPE_GAIN * (chosen - steady_ref[span, :]), 0.0, 1.0)
            mass = population_ref[span, :]
            mass_low[span, :] = mass * share
            mass_high[span, :] = mass * (1.0 - share)

    lanes = 2 * liq_n
    sub = iota((lanes, liq_rows), 0)
    lane = iota((lanes, liq_rows), 1)
    sub_block = jnp.where(sub < liq_n, sub, sub - liq_n)
    lane_row = iota((liq_rows, liq_rows), 0)
    per_tile = TILE // group

    def scatter_tile(d, tile):
        span = pl.ds(pl.multiple_of(tile * TILE, TILE), TILE)
        low_t, high_t, hi_t, lo_t = mass_low[span, :], mass_high[span, :], target_hi[span, :], target_lo[span, :]
        for zz in range(per_tile):
            z = tile * per_tile + zz
            totals = []
            for a in range(ill_rows):
                k = zz * group + d * ill_rows + a
                both = jnp.where(sub < liq_n, low_t[k : k + 1, :], high_t[k : k + 1, :])
                both = jnp.where(hi_t[k : k + 1, :] == sub_block, both, 0.0)
                rounded = both.astype(jnp.bfloat16).astype(jnp.float32)
                parts = jnp.concatenate([both, both - rounded], axis=0).astype(jnp.bfloat16)
                hot = as_float(lane_row == lo_t[k : k + 1, :]).astype(jnp.bfloat16)
                placed = lax.dot_general(parts, hot, NT, preferred_element_type=jnp.float32)
                placed = placed[:lanes] + placed[lanes:]
                moved = pltpu.roll(placed, 1, 1)
                same = pltpu.roll(moved, liq_n, 0)
                prior = pltpu.roll(moved, liq_n + 1, 0)
                totals.append(placed + jnp.where(lane > 0, same, jnp.where(sub > 0, prior, 0.0)))
            for dest in range(ill_n * ill_rows):
                out = None
                for a in range(ill_rows):
                    here = as_float(ill_target_ref[d * ill_rows + a, z] == dest) * totals[a]
                    out = here if out is None else out + here
                base = (d * ill_n + dest // ill_rows) * liq_n * plane_rows + z * ill_rows + dest % ill_rows
                terms[pl.ds(base, liq_n, stride=plane_rows), :] = out[:liq_n]

    def scatter(d, half):
        def step(pair, carry):
            scatter_tile(d, halves[half].start + 2 * pair)
            scatter_tile(d, halves[half].start + 2 * pair + 1)
            return carry

        lax.fori_loop(0, tiles // 4, step, 0)

    def send_owners(d):
        for step in range(1, ill_n):
            terms_copy(d, step).wait_recv()
        for h in range(liq_n):
            start = pl.multiple_of(((d * ill_n + ill_me) * liq_n + h) * plane_rows, TILE)
            total = terms[pl.ds(start, plane_rows), :]
            for step in range(1, ill_n):
                total = total + terms_in[d * (ill_n - 1) + step - 1, pl.ds(h * plane_rows, plane_rows), :]
            owner_sum[d * liq_n + h] = total
        for step in far_first:
            owner_copy(d, step).start()

    def collect(d):
        for step in far_first:
            owner_copy(d, step).wait_recv()
        total = owner_sum[d * liq_n + liq_me]
        for step in range(1, liq_n):
            total = total + owner_in[d * (liq_n - 1) + step - 1]
        settled[pl.ds(d * plane_rows, plane_rows), :] = total
        return total

    def second_policy(half):
        for step in far_first:
            pencil_copy(1, half, step).wait_recv()
        for tile in halves[half]:
            consumption_ref[pl.ds(tile * TILE, TILE), :] = interpolate(1, tile)

    first_policy(0)
    scatter(0, 0)
    first_policy(1)
    value_copy(1, value_two).start()
    scatter(0, 1)
    for step in range(1, ill_n):
        terms_copy(0, step).start()
    value_copy(1, value_two).wait_recv()
    drifted = dot(second_mat[...], value_two[...]) + dot(second_up[...], near_value[1])
    pencil[liq_n + liq_me] = lax.rsqrt(drifted)
    for step in far_first:
        pencil_copy(1, 0, step).start()
    for d in range(1, durables):
        scatter(d, 0)
        if d == 1:
            send_owners(0)
        scatter(d, 1)
        for step in range(1, ill_n):
            terms_copy(d, step).start()
    for d in range(1, durables):
        send_owners(d)
    for step in far_first:
        pencil_copy(1, 1, step).start()

    depart_copy = pltpu.make_async_remote_copy(
        src_ref=depart, dst_ref=depart_in, send_sem=depart_send.at[0], recv_sem=depart_recv.at[0],
        device_id={"dur": jnp.maximum(dur_me - 1, 0)}, device_id_type=MESH_ID,
    )

    second_policy(0)
    depart[...] = (1.0 - stay[0]) * collect(0)

    @pl.when(dur_me > 0)
    def _():
        depart_copy.start()

    for d in range(1, durables):
        collect(d)
    next_ref[...] = dot(next_mat[...], settled[...])
    second_policy(1)
    stores = [
        pltpu.make_async_copy(consumption_ref, consumption_hbm, store_sem.at[0]),
        pltpu.make_async_copy(next_ref, next_hbm, store_sem.at[1]),
    ]
    stores[0].start()

    @pl.when(dur_me < dur_n - 1)
    def _():
        depart_copy.wait_recv()
        next_ref[...] += dot(next_in[...], depart_in[...])

    stores[1].start()

    value_copy(0, value_ref).wait_send()
    value_copy(1, value_two).wait_send()
    for step in range(1, liq_n):
        for k in range(2):
            for half in range(2):
                pencil_copy(k, half, step).wait_send()
        for d in range(durables):
            owner_copy(d, step).wait_send()
    for step in range(1, ill_n):
        for d in range(durables):
            terms_copy(d, step).wait_send()

    @pl.when(dur_me > 0)
    def _():
        depart_copy.wait_send()

    stores[0].wait()
    stores[1].wait()


def body(
    marginal_value,
    transition,
    discount_shock,
    illiquid_drift,
    durable_keep,
    bracket_index,
    bracket_weight,
    steady_consumption,
    lottery_weight,
    liquid_target,
    illiquid_target,
    population,
):
    shape = marginal_value.shape
    incomes, durables, ill_rows, liq_rows = shape
    liq_n, ill_n, dur_n = (lax.axis_size(name) for name in ("liq", "ill", "dur"))
    rows = incomes * durables * ill_rows
    plane_rows = incomes * ill_rows
    flat = lambda x: x.reshape(rows, liq_rows)
    anywhere = pl.BlockSpec(memory_space=pl.ANY)
    smem = pl.BlockSpec(memory_space=pltpu.SMEM)
    f32 = jnp.float32
    block = (rows, liq_rows)
    dma = pltpu.SemaphoreType.DMA
    result = jax.ShapeDtypeStruct(block, f32)
    dims = (incomes, durables, ill_rows, liq_rows, liq_n, ill_n, dur_n)
    outs = pl.pallas_call(
        functools.partial(kernel, dims),
        out_shape=(result, result),
        in_specs=[anywhere, anywhere, anywhere, smem, smem] + [anywhere] * 5 + [smem, anywhere],
        out_specs=(anywhere, anywhere),
        scratch_shapes=[
            pltpu.VMEM(block, f32),
            pltpu.VMEM((incomes, incomes), f32),
            pltpu.VMEM((1, incomes), f32),
            pltpu.VMEM(block, jnp.int32),
            pltpu.VMEM(block, f32),
            pltpu.VMEM(block, f32),
            pltpu.VMEM(block, f32),
            pltpu.VMEM(block, jnp.int32),
            pltpu.VMEM(block, f32),
            pltpu.VMEM(block, f32),
            pltpu.VMEM(block, f32),
            dma((9,)),
            dma((2,)),
            pltpu.VMEM((rows, rows), f32),
            pltpu.VMEM((rows, rows), f32),
            pltpu.VMEM((rows, rows), f32),
            pltpu.VMEM((rows, rows), f32),
            pltpu.VMEM((rows, rows), f32),
            pltpu.VMEM((rows, plane_rows), f32),
            pltpu.VMEM((2,) + block, f32),
            pltpu.VMEM(block, f32),
            pltpu.VMEM((2 * liq_n,) + block, f32),
            pltpu.VMEM(block, f32),
            pltpu.VMEM(block, f32),
            pltpu.VMEM(block, jnp.int32),
            pltpu.VMEM(block, jnp.int32),
            pltpu.VMEM((ill_n * liq_n * rows, liq_rows), f32),
            pltpu.VMEM((durables * (ill_n - 1), liq_n * plane_rows, liq_rows), f32),
            pltpu.VMEM((durables * liq_n, plane_rows, liq_rows), f32),
            pltpu.VMEM((durables * (liq_n - 1), plane_rows, liq_rows), f32),
            pltpu.VMEM(block, f32),
            pltpu.VMEM((plane_rows, liq_rows), f32),
            pltpu.VMEM((plane_rows, liq_rows), f32),
            dma((2,)),
            dma((2,)),
            dma((4 * liq_n,)),
            dma((4 * liq_n,)),
            dma((durables * (ill_n - 1),)),
            dma((durables * (ill_n - 1),)),
            dma((durables * (liq_n - 1),)),
            dma((durables * (liq_n - 1),)),
            dma((1,)),
            dma((1,)),
        ],
        compiler_params=pltpu.CompilerParams(collective_id=0, has_side_effects=True),
        name="window",
    )(
        flat(marginal_value),
        transition,
        discount_shock.reshape(1, incomes),
        illiquid_drift,
        durable_keep,
        flat(bracket_index),
        flat(bracket_weight),
        flat(steady_consumption),
        flat(lottery_weight),
        flat(liquid_target),
        jnp.transpose(illiquid_target, (1, 2, 0)).reshape(durables * ill_rows, incomes),
        flat(population),
    )
    return tuple(out.reshape(shape) for out in outs)


def solution(mesh):
    in_specs = (
        P(None, "dur", "ill", "liq"),
        P(),
        P(),
        P("ill"),
        P("dur"),
        P(None, "dur", "ill", "liq"),
        P(None, "dur", "ill", "liq"),
        P(None, "dur", "ill", "liq"),
        P(None, "dur", "ill", "liq"),
        P(None, "dur", "ill", "liq"),
        P(None, "dur", "ill"),
        P(None, "dur", "ill", "liq"),
    )
    out_specs = (P(None, "dur", "ill", "liq"), P(None, "dur", "ill", "liq"))
    return jax.shard_map(body, mesh=mesh, in_specs=in_specs, out_specs=out_specs, check_vma=False)
```

```python
import functools

import jax
import jax.numpy as jnp
from jax import lax
from jax.experimental import pallas as pl
from jax.experimental.pallas import tpu as pltpu
from jax.sharding import PartitionSpec as P

DISCOUNT = 0.96
GROSS_RATE = 1.01
SLOPE_GAIN = 0.5
HIGHEST_PREC = lax.Precision.HIGHEST
MESH_ID = pl.DeviceIdType.MESH
NT = (((1,), (1,)), ((), ()))
TILE = 8


def split_by(x, n):
    if n & (n - 1) == 0:
        return x >> (n.bit_length() - 1), x & (n - 1)
    return lax.div(x, jnp.int32(n)), lax.rem(x, jnp.int32(n))


def dot(a, b):
    return jnp.dot(a, b, precision=HIGHEST_PREC, preferred_element_type=jnp.float32)


def iota(shape, axis):
    return lax.broadcasted_iota(jnp.int32, shape, axis)


def as_float(flag):
    return jnp.where(flag, jnp.float32(1.0), jnp.float32(0.0))


def peer_of(me, step, n):
    if n & (n - 1):
        return lax.rem(me + step, n)
    out = me
    for bit in range(n.bit_length() - 1):
        if step >> bit & 1:
            out = out + (1 - 2 * lax.rem(lax.div(me, jnp.int32(1 << bit)), jnp.int32(2))) * (1 << bit)
    return out


def kernel(
    dims,
    value_hbm, transition_hbm, shock_hbm, drift_ref, keep_ref, index_hbm, weight_hbm,
    steady_hbm, lottery_hbm, target_hbm, ill_target_ref, population_hbm,
    consumption_ref, next_ref,
    value_ref, transition_ref, shock_ref, index_ref, weight_ref, steady_ref, lottery_ref, target_ref,
    population_ref, load_sem,
    first_mat, first_up, second_mat, second_up, next_mat, next_in,
    near_value, value_two, pencil, mass_low, mass_high, target_hi, target_lo,
    terms, terms_in, owner_sum, owner_in, settled, depart, depart_in,
    value_send, value_recv, pencil_send, pencil_recv, terms_send, terms_recv,
    owner_send, owner_recv, depart_send, depart_recv,
):
    incomes, durables, ill_rows, liq_rows, liq_n, ill_n, dur_n = dims
    group = durables * ill_rows
    rows = incomes * group
    half_rows = rows // 2
    plane_rows = incomes * ill_rows
    liq_me, ill_me, dur_me = (lax.axis_index(name) for name in ("liq", "ill", "dur"))
    far_first = range(liq_n - 1, 0, -1)

    barrier = pltpu.get_barrier_semaphore()
    for step in far_first:
        pl.semaphore_signal(barrier, inc=1, device_id={"liq": peer_of(liq_me, step, liq_n)}, device_id_type=MESH_ID)
    for step in range(1, ill_n):
        pl.semaphore_signal(barrier, inc=1, device_id={"ill": peer_of(ill_me, step, ill_n)}, device_id_type=MESH_ID)

    @pl.when(dur_me > 0)
    def _():
        pl.semaphore_signal(barrier, inc=1, device_id={"dur": dur_me - 1}, device_id_type=MESH_ID)

    @pl.when(dur_me < dur_n - 1)
    def _():
        pl.semaphore_signal(barrier, inc=1, device_id={"dur": dur_me + 1}, device_id_type=MESH_ID)

    loads = [
        pltpu.make_async_copy(source, held, load_sem.at[slot])
        for slot, (source, held) in enumerate((
            (transition_hbm, transition_ref), (shock_hbm, shock_ref), (value_hbm, value_ref),
            (index_hbm, index_ref), (weight_hbm, weight_ref), (target_hbm, target_ref),
            (lottery_hbm, lottery_ref), (steady_hbm, steady_ref), (population_hbm, population_ref),
        ))
    ]
    for load in loads:
        load.start()
    loads[0].wait()
    loads[1].wait()

    transition = transition_ref[...]
    row_z, row_rest = split_by(iota((rows, rows), 0), group)
    col_z, col_rest = split_by(iota((rows, rows), 1), group)
    row_d, row_a = split_by(row_rest, ill_rows)
    col_d, col_a = split_by(col_rest, ill_rows)
    spread = as_float(split_by(iota((rows, incomes), 0), group)[0] == iota((rows, incomes), 1))
    spread_t = as_float(iota((incomes, rows), 0) == split_by(iota((incomes, rows), 1), group)[0])
    drift = jnp.zeros((rows, rows), jnp.float32)
    for a in range(ill_rows):
        drift = jnp.where(row_a == a, drift_ref[a], drift)
    is_last = as_float(ill_me == ill_n - 1)
    same_d = row_d == col_d
    top_row = row_a == ill_rows - 1
    local = jnp.where(col_a == row_a, drift, 0.0)
    local = local + jnp.where(col_a == row_a + 1, 1.0 - drift, 0.0)
    local = local + jnp.where(top_row & (col_a == ill_rows - 1), is_last * (1.0 - drift), 0.0)
    local = jnp.where(same_d, local, 0.0)
    upper = jnp.where(same_d & top_row & (col_a == 0), (1.0 - is_last) * (1.0 - drift), 0.0)
    constant = jnp.float32(DISCOUNT * GROSS_RATE)
    eye = iota((incomes, incomes), 0) == iota((incomes, incomes), 1)
    scaled = dot(jnp.where(eye, constant * shock_ref[...], 0.0), transition)
    wide = dot(dot(spread, scaled), spread_t)
    first_mat[...] = wide * local
    first_up[...] = wide * upper

    dur_peers = jnp.minimum(dur_me, 1) + jnp.minimum(dur_n - 1 - dur_me, 1)
    pl.semaphore_wait(barrier, liq_n - 1 + ill_n - 1 + dur_peers)

    ill_below = lax.rem(ill_me + ill_n - 1, ill_n)

    def value_copy(k, source):
        return pltpu.make_async_remote_copy(
            src_ref=source, dst_ref=near_value.at[k], send_sem=value_send.at[k],
            recv_sem=value_recv.at[k], device_id={"ill": ill_below}, device_id_type=MESH_ID,
        )

    def pencil_copy(k, half, step):
        slot = (k * 2 + half) * liq_n + step
        part = pencil.at[k * liq_n + liq_me, pl.ds(half * half_rows, half_rows)]
        return pltpu.make_async_remote_copy(
            src_ref=part, dst_ref=part, send_sem=pencil_send.at[slot], recv_sem=pencil_recv.at[slot],
            device_id={"liq": peer_of(liq_me, step, liq_n)}, device_id_type=MESH_ID,
        )

    def terms_copy(d, step):
        peer = peer_of(ill_me, step, ill_n)
        slot = d * (ill_n - 1) + step - 1
        return pltpu.make_async_remote_copy(
            src_ref=terms.at[pl.ds((d * ill_n + peer) * (liq_n * plane_rows), liq_n * plane_rows)],
            dst_ref=terms_in.at[slot], send_sem=terms_send.at[slot], recv_sem=terms_recv.at[slot],
            device_id={"ill": peer}, device_id_type=MESH_ID,
        )

    def owner_copy(d, step):
        peer = peer_of(liq_me, step, liq_n)
        slot = d * (liq_n - 1) + step - 1
        return pltpu.make_async_remote_copy(
            src_ref=owner_sum.at[d * liq_n + peer], dst_ref=owner_in.at[slot],
            send_sem=owner_send.at[slot], recv_sem=owner_recv.at[slot],
            device_id={"liq": peer}, device_id_type=MESH_ID,
        )

    loads[2].wait()
    value_copy(0, value_ref).start()
    drifted = dot(first_mat[...], value_ref[...])
    value_copy(0, value_ref).wait_recv()
    drifted = drifted + dot(first_up[...], near_value[0])
    pencil[liq_me] = lax.rsqrt(drifted)
    for half in range(2):
        for step in far_first:
            pencil_copy(0, half, step).start()

    wide = constant * dot(dot(spread, transition), spread_t)
    second_mat[...] = wide * local
    second_up[...] = wide * upper

    first_d = as_float(dur_me == 0)
    stay = [keep_ref[d] for d in range(durables)]
    stay[0] = first_d + (1.0 - first_d) * stay[0]
    back_d, back_rest = split_by(iota((rows, rows), 1), plane_rows)
    back_a = split_by(back_rest, ill_rows)[1]
    stays = jnp.zeros((rows, rows), jnp.float32)
    for d in range(durables):
        stays = jnp.where(back_d == d, stay[d], stays)
    mix = jnp.where(back_d == row_d, stays, 0.0) + jnp.where(back_d == row_d + 1, 1.0 - stays, 0.0)
    mix = jnp.where(back_a == row_a, mix, 0.0)
    back_z = split_by(split_by(iota((incomes, rows), 1), plane_rows)[1], ill_rows)[0]
    turned = lax.dot_general(spread, transition, NT, precision=HIGHEST_PREC, preferred_element_type=jnp.float32)
    wide = dot(turned, as_float(iota((incomes, rows), 0) == back_z))
    next_mat[...] = wide * mix
    in_z, in_a = split_by(iota((incomes, plane_rows), 1), ill_rows)
    wide = dot(turned, as_float(iota((incomes, plane_rows), 0) == in_z))
    in_row = split_by(iota((rows, plane_rows), 0), group)[1]
    in_row_d, in_row_a = split_by(in_row, ill_rows)
    in_col_a = split_by(iota((rows, plane_rows), 1), ill_rows)[1]
    next_in[...] = jnp.where((in_row_d == durables - 1) & (in_row_a == in_col_a), wide, 0.0)

    def block_of(position):
        block = jnp.zeros(position.shape, jnp.int32)
        for h in range(1, liq_n):
            block = block + jnp.where(position >= h * liq_rows, 1, 0)
        return block, position - block * liq_rows

    for load in loads[3:]:
        load.wait()
    target_hi[...], target_lo[...] = block_of(target_ref[...])

    def interpolate(k, tile):
        span = pl.ds(tile * TILE, TILE)
        index = index_ref[span, :]
        low_block, low_lane = block_of(index)
        high_block, high_lane = block_of(index + 1)
        low = high = None
        for h in range(liq_n):
            block = pencil[k * liq_n + h, span, :]
            low_h = jnp.take_along_axis(block, low_lane, axis=1, mode="promise_in_bounds")
            high_h = jnp.take_along_axis(block, high_lane, axis=1, mode="promise_in_bounds")
            low = low_h if h == 0 else jnp.where(low_block == h, low_h, low)
            high = high_h if h == 0 else jnp.where(high_block == h, high_h, high)
        weight = weight_ref[span, :]
        return weight * low + (1.0 - weight) * high

    tiles = rows // TILE
    halves = (range(tiles // 2), range(tiles // 2, tiles))

    def first_policy(half):
        for step in far_first:
            pencil_copy(0, half, step).wait_recv()
        for tile in halves[half]:
            span = pl.ds(tile * TILE, TILE)
            chosen = interpolate(0, tile)
            value_two[span, :] = GROSS_RATE / (chosen * chosen)
            share = jnp.clip(lottery_ref[span, :] + SLOPE_GAIN * (chosen - steady_ref[span, :]), 0.0, 1.0)
            mass = population_ref[span, :]
            mass_low[span, :] = mass * share
            mass_high[span, :] = mass * (1.0 - share)

    lanes = 2 * liq_n
    sub = iota((lanes, liq_rows), 0)
    lane = iota((lanes, liq_rows), 1)
    sub_block = jnp.where(sub < liq_n, sub, sub - liq_n)
    lane_row = iota((liq_rows, liq_rows), 0)
    per_tile = TILE // group

    def scatter_tile(d, tile):
        span = pl.ds(pl.multiple_of(tile * TILE, TILE), TILE)
        low_t, high_t, hi_t, lo_t = mass_low[span, :], mass_high[span, :], target_hi[span, :], target_lo[span, :]
        for zz in range(per_tile):
            z = tile * per_tile + zz
            totals = []
            for a in range(ill_rows):
                k = zz * group + d * ill_rows + a
                both = jnp.where(sub < liq_n, low_t[k : k + 1, :], high_t[k : k + 1, :])
                both = jnp.where(hi_t[k : k + 1, :] == sub_block, both, 0.0)
                rounded = both.astype(jnp.bfloat16).astype(jnp.float32)
                parts = jnp.concatenate([both, both - rounded], axis=0).astype(jnp.bfloat16)
                hot = as_float(lane_row == lo_t[k : k + 1, :]).astype(jnp.bfloat16)
                placed = lax.dot_general(parts, hot, NT, preferred_element_type=jnp.float32)
                placed = placed[:lanes] + placed[lanes:]
                moved = pltpu.roll(placed, 1, 1)
                same = pltpu.roll(moved, liq_n, 0)
                prior = pltpu.roll(moved, liq_n + 1, 0)
                totals.append(placed + jnp.where(lane > 0, same, jnp.where(sub > 0, prior, 0.0)))
            for dest in range(ill_n * ill_rows):
                out = None
                for a in range(ill_rows):
                    here = as_float(ill_target_ref[d * ill_rows + a, z] == dest) * totals[a]
                    out = here if out is None else out + here
                base = (d * ill_n + dest // ill_rows) * liq_n * plane_rows + z * ill_rows + dest % ill_rows
                terms[pl.ds(base, liq_n, stride=plane_rows), :] = out[:liq_n]

    def scatter(d, half):
        def step(pair, carry):
            scatter_tile(d, halves[half].start + 2 * pair)
            scatter_tile(d, halves[half].start + 2 * pair + 1)
            return carry

        lax.fori_loop(0, tiles // 4, step, 0)

    def send_owners(d):
        for step in range(1, ill_n):
            terms_copy(d, step).wait_recv()
        for h in range(liq_n):
            start = pl.multiple_of(((d * ill_n + ill_me) * liq_n + h) * plane_rows, TILE)
            total = terms[pl.ds(start, plane_rows), :]
            for step in range(1, ill_n):
                total = total + terms_in[d * (ill_n - 1) + step - 1, pl.ds(h * plane_rows, plane_rows), :]
            owner_sum[d * liq_n + h] = total
        for step in far_first:
            owner_copy(d, step).start()

    def collect(d):
        for step in far_first:
            owner_copy(d, step).wait_recv()
        total = owner_sum[d * liq_n + liq_me]
        for step in range(1, liq_n):
            total = total + owner_in[d * (liq_n - 1) + step - 1]
        settled[pl.ds(d * plane_rows, plane_rows), :] = total
        return total

    def second_policy(half):
        for step in far_first:
            pencil_copy(1, half, step).wait_recv()
        for tile in halves[half]:
            consumption_ref[pl.ds(tile * TILE, TILE), :] = interpolate(1, tile)

    first_policy(0)
    scatter(0, 0)
    first_policy(1)
    value_copy(1, value_two).start()
    scatter(0, 1)
    for step in range(1, ill_n):
        terms_copy(0, step).start()
    value_copy(1, value_two).wait_recv()
    drifted = dot(second_mat[...], value_two[...]) + dot(second_up[...], near_value[1])
    pencil[liq_n + liq_me] = lax.rsqrt(drifted)
    for step in far_first:
        pencil_copy(1, 0, step).start()
    for d in range(1, durables):
        scatter(d, 0)
        if d == 1:
            send_owners(0)
        scatter(d, 1)
        for step in range(1, ill_n):
            terms_copy(d, step).start()
    for d in range(1, durables):
        send_owners(d)
    for step in far_first:
        pencil_copy(1, 1, step).start()

    depart_copy = pltpu.make_async_remote_copy(
        src_ref=depart, dst_ref=depart_in, send_sem=depart_send.at[0], recv_sem=depart_recv.at[0],
        device_id={"dur": jnp.maximum(dur_me - 1, 0)}, device_id_type=MESH_ID,
    )

    second_policy(0)
    depart[...] = (1.0 - stay[0]) * collect(0)

    @pl.when(dur_me > 0)
    def _():
        depart_copy.start()

    for d in range(1, durables):
        collect(d)
    next_ref[...] = dot(next_mat[...], settled[...])
    second_policy(1)

    @pl.when(dur_me < dur_n - 1)
    def _():
        depart_copy.wait_recv()
        next_ref[...] += dot(next_in[...], depart_in[...])

    value_copy(0, value_ref).wait_send()
    value_copy(1, value_two).wait_send()
    for step in range(1, liq_n):
        for k in range(2):
            for half in range(2):
                pencil_copy(k, half, step).wait_send()
        for d in range(durables):
            owner_copy(d, step).wait_send()
    for step in range(1, ill_n):
        for d in range(durables):
            terms_copy(d, step).wait_send()

    @pl.when(dur_me > 0)
    def _():
        depart_copy.wait_send()


def store(consumption_ref, next_ref, consumption_hbm, next_hbm, sem):
    copies = [
        pltpu.make_async_copy(consumption_ref, consumption_hbm, sem.at[0]),
        pltpu.make_async_copy(next_ref, next_hbm, sem.at[1]),
    ]
    for copy in copies:
        copy.start()
    for copy in copies:
        copy.wait()


def body(
    marginal_value,
    transition,
    discount_shock,
    illiquid_drift,
    durable_keep,
    bracket_index,
    bracket_weight,
    steady_consumption,
    lottery_weight,
    liquid_target,
    illiquid_target,
    population,
):
    shape = marginal_value.shape
    incomes, durables, ill_rows, liq_rows = shape
    liq_n, ill_n, dur_n = (lax.axis_size(name) for name in ("liq", "ill", "dur"))
    rows = incomes * durables * ill_rows
    plane_rows = incomes * ill_rows
    flat = lambda x: x.reshape(rows, liq_rows)
    anywhere = pl.BlockSpec(memory_space=pl.ANY)
    smem = pl.BlockSpec(memory_space=pltpu.SMEM)
    f32 = jnp.float32
    block = (rows, liq_rows)
    dma = pltpu.SemaphoreType.DMA
    vmem = pl.BlockSpec(memory_space=pltpu.VMEM)
    held = pltpu.VMEM(block, f32)
    result = jax.ShapeDtypeStruct(block, f32)
    dims = (incomes, durables, ill_rows, liq_rows, liq_n, ill_n, dur_n)
    outs = pl.pallas_call(
        functools.partial(kernel, dims),
        out_shape=(held, held),
        in_specs=[anywhere, anywhere, anywhere, smem, smem] + [anywhere] * 5 + [smem, anywhere],
        out_specs=(vmem, vmem),
        scratch_shapes=[
            pltpu.VMEM(block, f32),
            pltpu.VMEM((incomes, incomes), f32),
            pltpu.VMEM((1, incomes), f32),
            pltpu.VMEM(block, jnp.int32),
            pltpu.VMEM(block, f32),
            pltpu.VMEM(block, f32),
            pltpu.VMEM(block, f32),
            pltpu.VMEM(block, jnp.int32),
            pltpu.VMEM(block, f32),
            dma((9,)),
            pltpu.VMEM((rows, rows), f32),
            pltpu.VMEM((rows, rows), f32),
            pltpu.VMEM((rows, rows), f32),
            pltpu.VMEM((rows, rows), f32),
            pltpu.VMEM((rows, rows), f32),
            pltpu.VMEM((rows, plane_rows), f32),
            pltpu.VMEM((2,) + block, f32),
            pltpu.VMEM(block, f32),
            pltpu.VMEM((2 * liq_n,) + block, f32),
            pltpu.VMEM(block, f32),
            pltpu.VMEM(block, f32),
            pltpu.VMEM(block, jnp.int32),
            pltpu.VMEM(block, jnp.int32),
            pltpu.VMEM((ill_n * liq_n * rows, liq_rows), f32),
            pltpu.VMEM((durables * (ill_n - 1), liq_n * plane_rows, liq_rows), f32),
            pltpu.VMEM((durables * liq_n, plane_rows, liq_rows), f32),
            pltpu.VMEM((durables * (liq_n - 1), plane_rows, liq_rows), f32),
            pltpu.VMEM(block, f32),
            pltpu.VMEM((plane_rows, liq_rows), f32),
            pltpu.VMEM((plane_rows, liq_rows), f32),
            dma((2,)),
            dma((2,)),
            dma((4 * liq_n,)),
            dma((4 * liq_n,)),
            dma((durables * (ill_n - 1),)),
            dma((durables * (ill_n - 1),)),
            dma((durables * (liq_n - 1),)),
            dma((durables * (liq_n - 1),)),
            dma((1,)),
            dma((1,)),
        ],
        compiler_params=pltpu.CompilerParams(collective_id=0, has_side_effects=True),
        name="window",
    )(
        flat(marginal_value),
        transition,
        discount_shock.reshape(1, incomes),
        illiquid_drift,
        durable_keep,
        flat(bracket_index),
        flat(bracket_weight),
        flat(steady_consumption),
        flat(lottery_weight),
        flat(liquid_target),
        jnp.transpose(illiquid_target, (1, 2, 0)).reshape(durables * ill_rows, incomes),
        flat(population),
    )
    outs = pl.pallas_call(
        store,
        out_shape=(result, result),
        in_specs=[vmem, vmem],
        out_specs=(anywhere, anywhere),
        scratch_shapes=[dma((2,))],
        name="store",
    )(*(pltpu.with_memory_space_constraint(out, pltpu.VMEM) for out in outs))
    return tuple(out.reshape(shape) for out in outs)


def solution(mesh):
    in_specs = (
        P(None, "dur", "ill", "liq"),
        P(),
        P(),
        P("ill"),
        P("dur"),
        P(None, "dur", "ill", "liq"),
        P(None, "dur", "ill", "liq"),
        P(None, "dur", "ill", "liq"),
        P(None, "dur", "ill", "liq"),
        P(None, "dur", "ill", "liq"),
        P(None, "dur", "ill"),
        P(None, "dur", "ill", "liq"),
    )
    out_specs = (P(None, "dur", "ill", "liq"), P(None, "dur", "ill", "liq"))
    return jax.shard_map(body, mesh=mesh, in_specs=in_specs, out_specs=out_specs, check_vma=False)
```

```python
import functools

import jax
import jax.numpy as jnp
from jax import lax
from jax.experimental import pallas as pl
from jax.experimental.pallas import tpu as pltpu
from jax.sharding import PartitionSpec as P

DISCOUNT = 0.96
GROSS_RATE = 1.01
SLOPE_GAIN = 0.5
HIGHEST_PREC = lax.Precision.HIGHEST
MESH_ID = pl.DeviceIdType.MESH
NT = (((1,), (1,)), ((), ()))
TILE = 8


def split_by(x, n):
    if n & (n - 1) == 0:
        return x >> (n.bit_length() - 1), x & (n - 1)
    return lax.div(x, jnp.int32(n)), lax.rem(x, jnp.int32(n))


def dot(a, b):
    return jnp.dot(a, b, precision=HIGHEST_PREC, preferred_element_type=jnp.float32)


def iota(shape, axis):
    return lax.broadcasted_iota(jnp.int32, shape, axis)


def as_float(flag):
    return jnp.where(flag, jnp.float32(1.0), jnp.float32(0.0))


def peer_of(me, step, n):
    if n & (n - 1):
        return lax.rem(me + step, n)
    out = me
    for bit in range(n.bit_length() - 1):
        if step >> bit & 1:
            out = out + (1 - 2 * lax.rem(lax.div(me, jnp.int32(1 << bit)), jnp.int32(2))) * (1 << bit)
    return out


def kernel(
    dims,
    value_hbm, transition_hbm, shock_hbm, drift_hbm, keep_hbm, index_hbm, weight_hbm,
    steady_hbm, lottery_hbm, target_hbm, ill_target_hbm, population_hbm,
    consumption_ref, next_ref,
    value_ref, transition_ref, shock_ref, index_ref, weight_ref, steady_ref, lottery_ref, target_ref,
    population_ref, drift_ref, keep_ref, ill_target_ref, load_sem,
    first_mat, first_up, second_mat, second_up, next_mat, next_in,
    near_value, value_two, pencil, mass_low, mass_high, target_hi, target_lo,
    placed_rows, terms, terms_in, owner_sum, owner_in, settled, depart, depart_in,
    value_send, value_recv, pencil_send, pencil_recv, terms_send, terms_recv,
    owner_send, owner_recv, depart_send, depart_recv,
):
    incomes, durables, ill_rows, liq_rows, liq_n, ill_n, dur_n = dims
    group = durables * ill_rows
    rows = incomes * group
    half_rows = rows // 2
    plane_rows = incomes * ill_rows
    liq_me, ill_me, dur_me = (lax.axis_index(name) for name in ("liq", "ill", "dur"))
    far_first = range(liq_n - 1, 0, -1)

    barrier = pltpu.get_barrier_semaphore()
    for step in far_first:
        pl.semaphore_signal(barrier, inc=1, device_id={"liq": peer_of(liq_me, step, liq_n)}, device_id_type=MESH_ID)
    for step in range(1, ill_n):
        pl.semaphore_signal(barrier, inc=1, device_id={"ill": peer_of(ill_me, step, ill_n)}, device_id_type=MESH_ID)

    @pl.when(dur_me > 0)
    def _():
        pl.semaphore_signal(barrier, inc=1, device_id={"dur": dur_me - 1}, device_id_type=MESH_ID)

    @pl.when(dur_me < dur_n - 1)
    def _():
        pl.semaphore_signal(barrier, inc=1, device_id={"dur": dur_me + 1}, device_id_type=MESH_ID)

    loads = [
        pltpu.make_async_copy(source, held, load_sem.at[slot])
        for slot, (source, held) in enumerate((
            (transition_hbm, transition_ref), (shock_hbm, shock_ref), (drift_hbm, drift_ref), (value_hbm, value_ref),
            (keep_hbm, keep_ref), (ill_target_hbm, ill_target_ref),
            (index_hbm, index_ref), (weight_hbm, weight_ref), (target_hbm, target_ref),
            (lottery_hbm, lottery_ref), (steady_hbm, steady_ref), (population_hbm, population_ref),
        ))
    ]
    for load in loads:
        load.start()
    for load in loads[:3]:
        load.wait()

    transition = transition_ref[...]
    row_z, row_rest = split_by(iota((rows, rows), 0), group)
    col_z, col_rest = split_by(iota((rows, rows), 1), group)
    row_d, row_a = split_by(row_rest, ill_rows)
    col_d, col_a = split_by(col_rest, ill_rows)
    spread = as_float(split_by(iota((rows, incomes), 0), group)[0] == iota((rows, incomes), 1))
    spread_t = as_float(iota((incomes, rows), 0) == split_by(iota((incomes, rows), 1), group)[0])
    drift = jnp.zeros((rows, rows), jnp.float32)
    for a in range(ill_rows):
        drift = jnp.where(row_a == a, drift_ref[a], drift)
    is_last = as_float(ill_me == ill_n - 1)
    same_d = row_d == col_d
    top_row = row_a == ill_rows - 1
    local = jnp.where(col_a == row_a, drift, 0.0)
    local = local + jnp.where(col_a == row_a + 1, 1.0 - drift, 0.0)
    local = local + jnp.where(top_row & (col_a == ill_rows - 1), is_last * (1.0 - drift), 0.0)
    local = jnp.where(same_d, local, 0.0)
    upper = jnp.where(same_d & top_row & (col_a == 0), (1.0 - is_last) * (1.0 - drift), 0.0)
    constant = jnp.float32(DISCOUNT * GROSS_RATE)
    eye = iota((incomes, incomes), 0) == iota((incomes, incomes), 1)
    scaled = dot(jnp.where(eye, constant * shock_ref[...], 0.0), transition)
    wide = dot(dot(spread, scaled), spread_t)
    first_mat[...] = wide * local
    first_up[...] = wide * upper

    dur_peers = jnp.minimum(dur_me, 1) + jnp.minimum(dur_n - 1 - dur_me, 1)
    pl.semaphore_wait(barrier, liq_n - 1 + ill_n - 1 + dur_peers)

    ill_below = lax.rem(ill_me + ill_n - 1, ill_n)

    def value_copy(k, source):
        return pltpu.make_async_remote_copy(
            src_ref=source, dst_ref=near_value.at[k], send_sem=value_send.at[k],
            recv_sem=value_recv.at[k], device_id={"ill": ill_below}, device_id_type=MESH_ID,
        )

    def pencil_copy(k, half, step):
        slot = (k * 2 + half) * liq_n + step
        part = pencil.at[k * liq_n + liq_me, pl.ds(half * half_rows, half_rows)]
        return pltpu.make_async_remote_copy(
            src_ref=part, dst_ref=part, send_sem=pencil_send.at[slot], recv_sem=pencil_recv.at[slot],
            device_id={"liq": peer_of(liq_me, step, liq_n)}, device_id_type=MESH_ID,
        )

    def pencil_relay(half):
        near, far = (1, 2) if half == 0 else (2, 1)
        slot = (2 + half) * liq_n
        part = pencil.at[liq_n + peer_of(liq_me, near, liq_n), pl.ds(half * half_rows, half_rows)]
        return pltpu.make_async_remote_copy(
            src_ref=part, dst_ref=part, send_sem=pencil_send.at[slot], recv_sem=pencil_recv.at[slot],
            device_id={"liq": peer_of(liq_me, far, liq_n)}, device_id_type=MESH_ID,
        )

    relayed = liq_n == 4
    if relayed:
        early, late = [(0, 1), (1, 2)], [(1, 1), (0, 2)]
    else:
        early, late = [(0, step) for step in far_first], [(1, step) for step in far_first]

    def terms_copy(d, step):
        peer = peer_of(ill_me, step, ill_n)
        slot = d * (ill_n - 1) + step - 1
        return pltpu.make_async_remote_copy(
            src_ref=terms.at[pl.ds((d * ill_n + peer) * (liq_n * plane_rows), liq_n * plane_rows)],
            dst_ref=terms_in.at[slot], send_sem=terms_send.at[slot], recv_sem=terms_recv.at[slot],
            device_id={"ill": peer}, device_id_type=MESH_ID,
        )

    def owner_copy(d, step):
        peer = peer_of(liq_me, step, liq_n)
        slot = d * (liq_n - 1) + step - 1
        return pltpu.make_async_remote_copy(
            src_ref=owner_sum.at[d * liq_n + peer], dst_ref=owner_in.at[slot],
            send_sem=owner_send.at[slot], recv_sem=owner_recv.at[slot],
            device_id={"liq": peer}, device_id_type=MESH_ID,
        )

    loads[3].wait()
    value_copy(0, value_ref).start()
    drifted = dot(first_mat[...], value_ref[...])
    value_copy(0, value_ref).wait_recv()
    drifted = drifted + dot(first_up[...], near_value[0])
    pencil[liq_me] = lax.rsqrt(drifted)
    for half in range(2):
        for step in far_first:
            pencil_copy(0, half, step).start()

    wide = constant * dot(dot(spread, transition), spread_t)
    second_mat[...] = wide * local
    second_up[...] = wide * upper

    for load in loads[4:]:
        load.wait()

    first_d = as_float(dur_me == 0)
    stay = [keep_ref[d] for d in range(durables)]
    stay[0] = first_d + (1.0 - first_d) * stay[0]
    back_d, back_rest = split_by(iota((rows, rows), 1), plane_rows)
    back_a = split_by(back_rest, ill_rows)[1]
    stays = jnp.zeros((rows, rows), jnp.float32)
    for d in range(durables):
        stays = jnp.where(back_d == d, stay[d], stays)
    mix = jnp.where(back_d == row_d, stays, 0.0) + jnp.where(back_d == row_d + 1, 1.0 - stays, 0.0)
    mix = jnp.where(back_a == row_a, mix, 0.0)
    back_z = split_by(split_by(iota((incomes, rows), 1), plane_rows)[1], ill_rows)[0]
    turned = lax.dot_general(spread, transition, NT, precision=HIGHEST_PREC, preferred_element_type=jnp.float32)
    wide = dot(turned, as_float(iota((incomes, rows), 0) == back_z))
    next_mat[...] = wide * mix
    in_z, in_a = split_by(iota((incomes, plane_rows), 1), ill_rows)
    wide = dot(turned, as_float(iota((incomes, plane_rows), 0) == in_z))
    in_row = split_by(iota((rows, plane_rows), 0), group)[1]
    in_row_d, in_row_a = split_by(in_row, ill_rows)
    in_col_a = split_by(iota((rows, plane_rows), 1), ill_rows)[1]
    next_in[...] = jnp.where((in_row_d == durables - 1) & (in_row_a == in_col_a), wide, 0.0)

    def block_of(position):
        block = jnp.zeros(position.shape, jnp.int32)
        for h in range(1, liq_n):
            block = block + jnp.where(position >= h * liq_rows, 1, 0)
        return block, position - block * liq_rows

    target_hi[...], lo = block_of(target_ref[...])
    target_lo[...] = lo.astype(jnp.float32)

    def interpolate(k, tile):
        span = pl.ds(tile * TILE, TILE)
        index = index_ref[span, :]
        low_block, low_lane = block_of(index)
        high_block, high_lane = block_of(index + 1)
        low = high = None
        for h in range(liq_n):
            block = pencil[k * liq_n + h, span, :]
            low_h = jnp.take_along_axis(block, low_lane, axis=1, mode="promise_in_bounds")
            high_h = jnp.take_along_axis(block, high_lane, axis=1, mode="promise_in_bounds")
            low = low_h if h == 0 else jnp.where(low_block == h, low_h, low)
            high = high_h if h == 0 else jnp.where(high_block == h, high_h, high)
        weight = weight_ref[span, :]
        return weight * low + (1.0 - weight) * high

    tiles = rows // TILE
    halves = (range(tiles // 2), range(tiles // 2, tiles))

    def first_policy(half):
        for step in far_first:
            pencil_copy(0, half, step).wait_recv()
        for tile in halves[half]:
            span = pl.ds(tile * TILE, TILE)
            chosen = interpolate(0, tile)
            value_two[span, :] = GROSS_RATE / (chosen * chosen)
            share = jnp.clip(lottery_ref[span, :] + SLOPE_GAIN * (chosen - steady_ref[span, :]), 0.0, 1.0)
            mass = population_ref[span, :]
            mass_low[span, :] = mass * share
            mass_high[span, :] = mass * (1.0 - share)

    lanes = 2 * liq_n
    sub = iota((lanes, liq_rows), 0)
    lane_at = iota((TILE, liq_rows), 1)
    sub_block = jnp.where(sub < liq_n, sub, sub - liq_n)
    lane_row = iota((liq_rows, liq_rows), 0).astype(jnp.float32).astype(jnp.bfloat16)
    one = jnp.ones((liq_rows, liq_rows), jnp.bfloat16)
    nil = jnp.zeros((liq_rows, liq_rows), jnp.bfloat16)
    per_tile = TILE // group

    def scatter_tile(d, tile):
        span = pl.ds(pl.multiple_of(tile * TILE, TILE), TILE)
        low_t, high_t, hi_t, lo_t = mass_low[span, :], mass_high[span, :], target_hi[span, :], target_lo[span, :]
        for zz in range(per_tile):
            z = tile * per_tile + zz
            totals = []
            for a in range(ill_rows):
                k = zz * group + d * ill_rows + a
                both = jnp.where(sub < liq_n, low_t[k : k + 1, :], high_t[k : k + 1, :])
                both = jnp.where(hi_t[k : k + 1, :] == sub_block, both, 0.0)
                rounded = both.astype(jnp.bfloat16).astype(jnp.float32)
                parts = jnp.concatenate([both, both - rounded], axis=0).astype(jnp.bfloat16)
                place = jnp.broadcast_to(lo_t[k : k + 1, :], (2 * TILE, liq_rows)).astype(jnp.bfloat16)
                place = jnp.concatenate([place] * (liq_rows // (2 * TILE)), axis=0)
                hot = jnp.where(lane_row == place, one, nil)
                placed = lax.dot_general(parts, hot, NT, preferred_element_type=jnp.float32)
                placed = placed[:lanes] + placed[lanes:]
                totals.append(placed)
            for dest in range(ill_n * ill_rows):
                out = None
                for a in range(ill_rows):
                    here = as_float(ill_target_ref[d * ill_rows + a, z] == dest) * totals[a]
                    out = here if out is None else out + here
                base = dest // ill_rows * lanes * plane_rows + z * ill_rows + dest % ill_rows
                placed_rows[pl.ds(base, lanes, stride=plane_rows), :] = out

    unroll = tiles // 2

    def scatter(d, half):
        def step(pair, carry):
            for turn in range(unroll):
                scatter_tile(d, halves[half].start + unroll * pair + turn)
            return carry

        lax.fori_loop(0, tiles // 2 // unroll, step, 0)

    def send_terms(d):
        for owner in range(ill_n):
            for piece in range(plane_rows // TILE):
                carried = None
                for h in range(liq_n):
                    low_at = (owner * lanes + h) * plane_rows + piece * TILE
                    low = placed_rows[pl.ds(low_at, TILE), :]
                    moved = pltpu.roll(placed_rows[pl.ds(low_at + liq_n * plane_rows, TILE), :], 1, 1)
                    edge = jnp.where(lane_at > 0, moved, 0.0 if carried is None else carried)
                    carried = moved
                    out_at = ((d * ill_n + owner) * liq_n + h) * plane_rows + piece * TILE
                    terms[pl.ds(out_at, TILE), :] = low + edge
        for step in range(1, ill_n):
            terms_copy(d, step).start()

    def send_owners(d):
        for step in range(1, ill_n):
            terms_copy(d, step).wait_recv()
        for h in range(liq_n):
            start = pl.multiple_of(((d * ill_n + ill_me) * liq_n + h) * plane_rows, TILE)
            total = terms[pl.ds(start, plane_rows), :]
            for step in range(1, ill_n):
                total = total + terms_in[d * (ill_n - 1) + step - 1, pl.ds(h * plane_rows, plane_rows), :]
            owner_sum[d * liq_n + h] = total
        for step in far_first:
            owner_copy(d, step).start()

    def collect(d):
        for step in far_first:
            owner_copy(d, step).wait_recv()
        total = owner_sum[d * liq_n + liq_me]
        for step in range(1, liq_n):
            total = total + owner_in[d * (liq_n - 1) + step - 1]
        settled[pl.ds(d * plane_rows, plane_rows), :] = total
        return total

    def second_policy():
        if relayed:
            for half in range(2):
                pencil_relay(half).wait_recv()
        else:
            for half, step in early:
                pencil_copy(1, half, step).wait_recv()
        for half, step in late:
            pencil_copy(1, half, step).wait_recv()
        for tile in range(tiles):
            consumption_ref[pl.ds(tile * TILE, TILE), :] = interpolate(1, tile)

    first_policy(0)
    scatter(0, 0)
    first_policy(1)
    value_copy(1, value_two).start()
    scatter(0, 1)
    send_terms(0)
    value_copy(1, value_two).wait_recv()
    drifted = dot(second_mat[...], value_two[...]) + dot(second_up[...], near_value[1])
    pencil[liq_n + liq_me] = lax.rsqrt(drifted)
    for half, step in early:
        pencil_copy(1, half, step).start()
    for d in range(1, durables):
        scatter(d, 0)
        if d == 1:
            send_owners(0)
            for half, step in late:
                pencil_copy(1, half, step).start()
        scatter(d, 1)
        send_terms(d)
    for d in range(1, durables):
        send_owners(d)
    if relayed:
        for half, step in early:
            pencil_copy(1, half, step).wait_recv()
        for half in range(2):
            pencil_relay(half).start()

    depart_copy = pltpu.make_async_remote_copy(
        src_ref=depart, dst_ref=depart_in, send_sem=depart_send.at[0], recv_sem=depart_recv.at[0],
        device_id={"dur": jnp.maximum(dur_me - 1, 0)}, device_id_type=MESH_ID,
    )

    depart[...] = (1.0 - stay[0]) * collect(0)

    @pl.when(dur_me > 0)
    def _():
        depart_copy.start()

    for d in range(1, durables):
        collect(d)
    next_ref[...] = dot(next_mat[...], settled[...])
    second_policy()

    @pl.when(dur_me < dur_n - 1)
    def _():
        depart_copy.wait_recv()
        next_ref[...] += dot(next_in[...], depart_in[...])

    value_copy(0, value_ref).wait_send()
    value_copy(1, value_two).wait_send()
    for step in range(1, liq_n):
        for half in range(2):
            pencil_copy(0, half, step).wait_send()
        for d in range(durables):
            owner_copy(d, step).wait_send()
    for half, step in early + late:
        pencil_copy(1, half, step).wait_send()
    if relayed:
        for half in range(2):
            pencil_relay(half).wait_send()
    for step in range(1, ill_n):
        for d in range(durables):
            terms_copy(d, step).wait_send()

    @pl.when(dur_me > 0)
    def _():
        depart_copy.wait_send()


def store(consumption_ref, next_ref, consumption_hbm, next_hbm, sem):
    copies = [
        pltpu.make_async_copy(consumption_ref, consumption_hbm, sem.at[0]),
        pltpu.make_async_copy(next_ref, next_hbm, sem.at[1]),
    ]
    for copy in copies:
        copy.start()
    for copy in copies:
        copy.wait()


def body(
    marginal_value,
    transition,
    discount_shock,
    illiquid_drift,
    durable_keep,
    bracket_index,
    bracket_weight,
    steady_consumption,
    lottery_weight,
    liquid_target,
    illiquid_target,
    population,
):
    shape = marginal_value.shape
    incomes, durables, ill_rows, liq_rows = shape
    liq_n, ill_n, dur_n = (lax.axis_size(name) for name in ("liq", "ill", "dur"))
    rows = incomes * durables * ill_rows
    plane_rows = incomes * ill_rows
    flat = lambda x: x.reshape(rows, liq_rows)
    anywhere = pl.BlockSpec(memory_space=pl.ANY)
    f32 = jnp.float32
    block = (rows, liq_rows)
    dma = pltpu.SemaphoreType.DMA
    vmem = pl.BlockSpec(memory_space=pltpu.VMEM)
    held = pltpu.VMEM(block, f32)
    result = jax.ShapeDtypeStruct(block, f32)
    dims = (incomes, durables, ill_rows, liq_rows, liq_n, ill_n, dur_n)
    outs = pl.pallas_call(
        functools.partial(kernel, dims),
        out_shape=(held, held),
        in_specs=[anywhere] * 12,
        out_specs=(vmem, vmem),
        scratch_shapes=[
            pltpu.VMEM(block, f32),
            pltpu.VMEM((incomes, incomes), f32),
            pltpu.VMEM((1, incomes), f32),
            pltpu.VMEM(block, jnp.int32),
            pltpu.VMEM(block, f32),
            pltpu.VMEM(block, f32),
            pltpu.VMEM(block, f32),
            pltpu.VMEM(block, jnp.int32),
            pltpu.VMEM(block, f32),
            pltpu.SMEM((ill_rows,), f32),
            pltpu.SMEM((durables,), f32),
            pltpu.SMEM((durables * ill_rows, incomes), jnp.int32),
            dma((12,)),
            pltpu.VMEM((rows, rows), f32),
            pltpu.VMEM((rows, rows), f32),
            pltpu.VMEM((rows, rows), f32),
            pltpu.VMEM((rows, rows), f32),
            pltpu.VMEM((rows, rows), f32),
            pltpu.VMEM((rows, plane_rows), f32),
            pltpu.VMEM((2,) + block, f32),
            pltpu.VMEM(block, f32),
            pltpu.VMEM((2 * liq_n,) + block, f32),
            pltpu.VMEM(block, f32),
            pltpu.VMEM(block, f32),
            pltpu.VMEM(block, jnp.int32),
            pltpu.VMEM(block, f32),
            pltpu.VMEM((2 * ill_n * liq_n * plane_rows, liq_rows), f32),
            pltpu.VMEM((ill_n * liq_n * rows, liq_rows), f32),
            pltpu.VMEM((durables * (ill_n - 1), liq_n * plane_rows, liq_rows), f32),
            pltpu.VMEM((durables * liq_n, plane_rows, liq_rows), f32),
            pltpu.VMEM((durables * (liq_n - 1), plane_rows, liq_rows), f32),
            pltpu.VMEM(block, f32),
            pltpu.VMEM((plane_rows, liq_rows), f32),
            pltpu.VMEM((plane_rows, liq_rows), f32),
            dma((2,)),
            dma((2,)),
            dma((4 * liq_n,)),
            dma((4 * liq_n,)),
            dma((durables * (ill_n - 1),)),
            dma((durables * (ill_n - 1),)),
            dma((durables * (liq_n - 1),)),
            dma((durables * (liq_n - 1),)),
            dma((1,)),
            dma((1,)),
        ],
        compiler_params=pltpu.CompilerParams(collective_id=0, has_side_effects=True),
        name="window",
    )(
        flat(marginal_value),
        transition,
        discount_shock.reshape(1, incomes),
        illiquid_drift,
        durable_keep,
        flat(bracket_index),
        flat(bracket_weight),
        flat(steady_consumption),
        flat(lottery_weight),
        flat(liquid_target),
        jnp.transpose(illiquid_target, (1, 2, 0)).reshape(durables * ill_rows, incomes),
        flat(population),
    )
    outs = pl.pallas_call(
        store,
        out_shape=(result, result),
        in_specs=[vmem, vmem],
        out_specs=(anywhere, anywhere),
        scratch_shapes=[dma((2,))],
        name="store",
    )(*(pltpu.with_memory_space_constraint(out, pltpu.VMEM) for out in outs))
    return tuple(out.reshape(shape) for out in outs)


def solution(mesh):
    in_specs = (
        P(None, "dur", "ill", "liq"),
        P(),
        P(),
        P("ill"),
        P("dur"),
        P(None, "dur", "ill", "liq"),
        P(None, "dur", "ill", "liq"),
        P(None, "dur", "ill", "liq"),
        P(None, "dur", "ill", "liq"),
        P(None, "dur", "ill", "liq"),
        P(None, "dur", "ill"),
        P(None, "dur", "ill", "liq"),
    )
    out_specs = (P(None, "dur", "ill", "liq"), P(None, "dur", "ill", "liq"))
    return jax.shard_map(body, mesh=mesh, in_specs=in_specs, out_specs=out_specs, check_vma=False)
```
